32 devices in a mesh: store: 8 (over y, x, core), vocab: 4 (over z).
Axes of the slice: x: 2, y: 2, z: 4, core: 2. Of those that a mesh axis runs over, the one named last changes fastest.
Arguments:
- hidden: bfloat16 [512, 4096], P('store')
- lm_head: bfloat16 [4096, 65536], P(None, ('store', 'vocab'))
- store_keys: bfloat16 [8192, 4096], P(('store', 'vocab'))
- values: int32 [8192], P(('store', 'vocab')), may hold values from 0 to 65535, as said below
- licences: int32 [8192], P(('store', 'vocab')), may hold values from 0 to 29, as said below
- allowed: int32 [512], replicated, may hold values from 1 to 1073741823, as said below
Outputs:
- log_probs: float32 [512, 65536], P(None, ('store', 'vocab'))
The draws below stay inside these ranges and needn't reach their ends.
Inputs may be any that keep to these rules, and one draw needn't show every extreme that they name: `values`: entry i holds a token t with t // 2048 = (i // 1024) * 4 + (i // 64) % 4: the entries of a device name tokens of the 8192 columns of its index along store, and its k-th run of 64 entries names tokens of the k-th 2048 columns of those. `licences`: some entry has licence 0. `allowed`: bit l of a position's word says whether licence l may be used; bit 0 is always set.
All inputs are finite; a program needn't handle non-finite values.
Results may differ from the reference program's by a relative error of at most 0.0003.
Values may be sent and summed in bfloat16 or wider, within the bound.
A program may use at most 128 MiB of HBM per device.

```python
import math
import jax
import jax.numpy as jnp
from jax import lax

D = 4096
VOCAB = 65536
QUERIES = 512
ENT_DEV = 256
NLIC = 30
ENTRIES = 8192
SLAB_COLS = 8192
OWN_COLS = 2048
BLOCK = 64


def key_row(key, index):
    row_key = jax.random.fold_in(jax.random.fold_in(key, 101), index)
    entries = jnp.clip(jax.random.normal(row_key, (D,), jnp.float32), -6.0, 6.0)
    shrink = 1.0 - 0.02 * index.astype(jnp.float32) / ENTRIES
    return entries * shrink


def head_column(key, column):
    column_key = jax.random.fold_in(jax.random.fold_in(key, 202), column)
    entries = jnp.clip(jax.random.normal(column_key, (D,), jnp.float32), -6.0, 6.0)
    growth = 3.5 * (0.8 + 0.4 * column.astype(jnp.float32) / VOCAB) / math.sqrt(D)
    return entries * growth


def draw_store_keys(key, part):
    rows = jax.vmap(lambda index: key_row(key, index))(jnp.arange(ENTRIES, dtype=jnp.int32))
    return rows.astype(jnp.bfloat16)


def draw_lm_head(key, part):
    columns = jax.vmap(lambda column: head_column(key, column))(jnp.arange(VOCAB, dtype=jnp.int32)).T
    return columns.astype(jnp.bfloat16)


def draw_hidden(key, part):
    base_key = jax.random.fold_in(key, 303)
    return jnp.clip(jax.random.normal(base_key, (QUERIES, D), jnp.float32), -6.0, 6.0).astype(jnp.bfloat16)


def draw_values(key, part):
    index = jnp.arange(ENTRIES, dtype=jnp.int32)
    per_slab = SLAB_COLS // OWN_COLS
    slab_index = index // (ENT_DEV * per_slab)
    within = index // BLOCK % per_slab
    offset = jax.random.randint(jax.random.fold_in(key, 7), (ENTRIES,), 0, OWN_COLS)
    offset = jnp.where(index == 0, 0, offset)
    offset = jnp.where(index == ENTRIES - 1, OWN_COLS - 1, offset)
    return ((slab_index * per_slab + within) * OWN_COLS + offset).astype(jnp.int32)


def draw_licences(key, part):
    index = jnp.arange(ENTRIES, dtype=jnp.int32)
    drawn = jax.random.randint(jax.random.fold_in(key, 8), (ENTRIES,), 0, NLIC)
    drawn = jnp.where(index == 0, 0, drawn)
    return jnp.where(index == 1, NLIC - 1, drawn).astype(jnp.int32)


def draw_allowed(key, part):
    index = jnp.arange(QUERIES, dtype=jnp.int32)
    words = jax.random.randint(jax.random.fold_in(key, 9), (QUERIES,), 0, 2 ** 30)
    words = jnp.bitwise_or(words, 1)
    words = jnp.where(index == 0, 2 ** 30 - 1, words)
    return jnp.where(index == 1, 1, words).astype(jnp.int32)


def setup_inputs(seed: int = 0) -> dict:
    key_of = jax.random.split(jax.random.key(seed), 7)
    return {
        "hidden": draw_hidden(jax.random.fold_in(key_of[6], 71), 0),
        "lm_head": draw_lm_head(jax.random.fold_in(key_of[6], 71), 0),
        "store_keys": draw_store_keys(jax.random.fold_in(key_of[6], 71), 0),
        "values": draw_values(jax.random.fold_in(key_of[6], 71), 0),
        "licences": draw_licences(jax.random.fold_in(key_of[6], 71), 0),
        "allowed": draw_allowed(jax.random.fold_in(key_of[6], 71), 0),
    }


NEG_FILL = -1e+30

def half_norm(block_rows):
    wide = block_rows.astype(jnp.float32)
    return 0.5 * lax.optimization_barrier(jnp.sum(wide * wide, axis=1)) / math.sqrt(D)

def reference(hidden, lm_head, store_keys, values, licences, allowed):
    logits = jnp.dot(hidden, lm_head, preferred_element_type=jnp.float32)
    lm_max = lax.optimization_barrier(jnp.max(logits, axis=1, keepdims=True))
    lm_total = lax.optimization_barrier(jnp.sum(jnp.exp(logits - lm_max), axis=1, keepdims=True))
    lm_log = logits - lm_max - jnp.log(lm_total)
    key_half = lax.map(half_norm, store_keys.reshape(-1, ENT_DEV, D)).reshape(-1)
    products = lax.dot_general(hidden, store_keys, (((1,), (1,)), ((), ())), preferred_element_type=jnp.float32)
    scores = products / math.sqrt(D) - key_half[None, :]
    permitted = jnp.bitwise_and(jnp.right_shift(allowed[:, None], licences[None, :]), 1) == 1
    masked = jnp.where(permitted, scores, NEG_FILL)
    knn_max = lax.optimization_barrier(jnp.max(masked, axis=1, keepdims=True))
    kernel = jnp.where(permitted, jnp.exp(masked - knn_max), 0.0)
    knn_total = lax.optimization_barrier(jnp.sum(kernel, axis=1, keepdims=True))
    knn_mass = jnp.zeros((QUERIES, VOCAB), jnp.float32).at[:, values].add(kernel)
    share = knn_mass / knn_total
    present = share > 0.0
    knn_log = jnp.where(present, jnp.log(jnp.where(present, share, 1.0)), -jnp.inf)
    return jnp.logaddexp(math.log(0.75) + lm_log, math.log(0.25) + knn_log)
```

```python
import functools
import math

import jax
import jax.numpy as jnp
from jax import lax
from jax.experimental import pallas as pl
from jax.experimental.pallas import tpu as pltpu
from jax.sharding import PartitionSpec as P

NEG_FILL = -1e30
LIFT = 40.0
DEPTH_CHUNK = 1024
MESH = pl.DeviceIdType.MESH
HOP_LAG = 3
USE_LAG = 4


def row_to_column(row, lanes=128):
    return jnp.broadcast_to(row, (lanes, row.shape[1])).T


def log_sum_exp(rows):
    top = functools.reduce(jnp.maximum, rows)
    total = functools.reduce(jnp.add, [jnp.exp(row - top) for row in rows])
    return top + jnp.log(total)


def mix(logits, share, shift):
    ours = logits - shift
    both = jnp.log(jnp.exp(ours + LIFT) + share) - LIFT
    return jnp.where(share > 0.0, both, ours)


def gather_kernel(
    S, V,
    hidden, lm_head, keys, values, licences, allowed,
    logits, share_out, shift_out,
    hid, head, key, lic, allow, val, scores, half, wsend, wrecv, weights, share, table, tok, tokcol, turn, turned,
    row_own, row_all, row_mid, row_end, row_every,
    own_sem, head_sem, key_sem, small_sem, gsend, grecv, tsend, trecv, wsend_sem, wrecv_sem,
    r1send, r1recv, r2send, r2recv, esend, erecv,
):
    R, D = hidden.shape
    C = lm_head.shape[1]
    E = keys.shape[0]
    H, K, RH, KC = hid.shape[0], hid.shape[2], hid.shape[3], hid.shape[4]
    Q = S * RH
    T = H * K
    B = E // V
    inverse_root = 1.0 / math.sqrt(D)
    s = lax.axis_index("store")
    v = lax.axis_index("vocab")

    def depth(k):
        return pl.ds(pl.multiple_of(k * KC, KC), KC)

    def place_of(i):
        return lax.div(i, K), lax.rem(i, K)

    def remote(src, dst, send, recv, store, vocab):
        return pltpu.make_async_remote_copy(
            src_ref=src, dst_ref=dst, send_sem=send, recv_sem=recv,
            device_id=(store, vocab), device_id_type=MESH,
        )

    def own_rows(i):
        h, k = place_of(i)
        return hidden.at[pl.ds(pl.multiple_of(h * RH, RH), RH), depth(k)]

    def block(i, origin):
        h, k = place_of(i)
        return hid.at[h, origin, k]

    def own_copy(i):
        return pltpu.make_async_copy(own_rows(i), block(i, s), own_sem.at[i])

    def head_copy(k):
        return pltpu.make_async_copy(lm_head.at[depth(k)], head.at[k], head_sem.at[k])

    def key_copy(k):
        return pltpu.make_async_copy(keys.at[:, depth(k)], key.at[k], key_sem.at[k])

    def loop(n, f):
        def step(k, carry):
            f(k)
            return carry
        lax.fori_loop(0, n, step, 0)

    store_peers = [lax.rem(s + j, S) for j in range(1, S)]
    vocab_peers = [lax.rem(v + j, V) for j in range(1, V)]
    vocab_from = [lax.rem(v + V - j, V) for j in range(1, V)]
    store_from = [lax.rem(s + S - j, S) for j in range(1, S)]

    barrier = pltpu.get_barrier_semaphore()
    for peer in store_peers:
        pl.semaphore_signal(barrier, inc=1, device_id=(peer, v), device_id_type=MESH)
    for peer in vocab_peers:
        pl.semaphore_signal(barrier, inc=1, device_id=(s, peer), device_id_type=MESH)

    small = [
        pltpu.make_async_copy(src, dst, small_sem.at[i])
        for i, (src, dst) in enumerate(((values, val), (licences, lic), (allowed, allow)))
    ]
    for copy in small:
        copy.start()
    loop(K, lambda k: key_copy(k).start())
    loop(T, lambda i: own_copy(i).start())

    pl.semaphore_wait(barrier, S + V - 2)

    tuned = H == 2
    if tuned:
        odd = lax.rem(v, 2)
        along_x = 2 - 4 * lax.rem(lax.div(s, 2), 2)
        along_y = 4 - 8 * lax.rem(lax.div(s, 4), 2)
        first = s + along_x * (1 - odd) + along_y * odd
        second = s + along_y * (1 - odd) + along_x * odd
        diagonal = s + along_x + along_y
        across = 1 - 2 * lax.rem(s, 2)
        pair = v + 1 - 2 * odd
        streams = [
            (s, (first, v), first),
            (first, (second, v), diagonal),
            (first, (s, pair), second),
            (s, (s + across, v), s + across),
            (first, (s + across, v), first + across),
            (diagonal, (s + across, v), diagonal + across),
            (second, (s + across, v), second + across),
        ]
    else:
        streams = [(s, (peer, v), source) for peer, source in zip(store_peers, store_from)]

    def send(t, i):
        origin, target, _ = streams[t]
        own = not tuned or t in (0, 3)
        src = own_rows(i) if own else block(i, origin)
        return remote(src, block(i, origin), gsend.at[t, i], grecv.at[t, i], *target)

    def arrive(t, i):
        _, target, origin = streams[t]
        return remote(block(i, origin), block(i, origin), gsend.at[t, i], grecv.at[t, i], *target)

    if tuned:
        def begin(i):
            send(0, i).start()
            send(3, i).start()
        loop(T, begin)
    else:
        for t in range(len(streams)):
            loop(T, lambda i: send(t, i).start())
    loop(K, lambda k: head_copy(k).start())

    for copy in small:
        copy.wait()
    tok[...] = jnp.broadcast_to(val[...], tok.shape)
    token_sends = []
    for j in range(1, V):
        copy = remote(tok, tokcol.at[v], tsend.at[j - 1], trecv.at[j - 1], s, vocab_peers[j - 1])
        copy.start()
        token_sends.append(copy)
    tokcol[v] = tok[...]

    def forward(i):
        if not tuned:
            return
        @pl.when(i < T)
        def _():
            arrive(0, i).wait_recv()
            send(1, i).start()
            send(2, i).start()
            send(4, i).start()

        @pl.when(jnp.logical_and(i >= HOP_LAG, i < T + HOP_LAG))
        def _():
            arrive(1, i - HOP_LAG).wait_recv()
            send(5, i - HOP_LAG).start()
            arrive(2, i - HOP_LAG).wait_recv()
            send(6, i - HOP_LAG).start()

    lag = USE_LAG if tuned else 0

    def ready(i):
        @pl.when(i < K)
        def _():
            head_copy(i).wait()
        own_copy(i).wait()
        for t in range(3, 7) if tuned else range(len(streams)):
            arrive(t, i).wait_recv()

    def states(i):
        h, k = place_of(i)
        return hid[h, :, k].reshape(Q, KC)

    def add_scores(i):
        h, k = place_of(i)
        scores[h] += lax.dot_general(
            key[k], states(i), (((1,), (1,)), ((), ())), preferred_element_type=jnp.float32
        )

    def add_logits(i):
        h, k = place_of(i)
        logits[h] += jnp.dot(
            states(i), head[k], preferred_element_type=jnp.float32
        ).reshape(S, RH, C)

    def norm_step(k):
        key_copy(k).wait()
        wide = key[k].astype(jnp.float32)
        square = wide * wide
        half[...] += functools.reduce(
            jnp.add, [square[:, i:i + 128] for i in range(0, KC, 128)]
        )

    def gather_step(i, carry):
        forward(i)
        ready(i - lag)
        add_scores(i - lag)
        add_logits(i - lag)
        return carry

    first_col = (s * V + v) * C
    half[...] = jnp.zeros_like(half)
    scores[...] = jnp.zeros_like(scores)
    forward(0)
    loop(K, norm_step)
    forward(1)
    logits[...] = jnp.zeros_like(logits)
    turned[...] = row_to_column(allow[...])
    half[...] = jnp.broadcast_to(jnp.sum(half[...], axis=1, keepdims=True), half.shape)
    allowed_row = [
        jnp.concatenate(
            [turned[o * R + h * RH:o * R + (h + 1) * RH, :] for o in range(S)], axis=0
        ).T[0:1, :]
        for h in range(H)
    ]
    forward(2)
    for j in range(1, V):
        slot = tokcol.at[vocab_from[j - 1]]
        remote(slot, slot, tsend.at[j - 1], trecv.at[j - 1], s, vocab_peers[j - 1]).wait_recv()
    for u in range(V):
        turn[...] = row_to_column(tokcol[u, 0:1, :])
        mine = turn[pl.ds(pl.multiple_of(v * B, B), B), 0:1] - first_col
        columns = lax.broadcasted_iota(jnp.int32, (B, C), 1)
        table[u * B:(u + 1) * B, :] = jnp.where(mine == columns, 1.0, 0.0).astype(jnp.bfloat16)
    turn[...] = row_to_column(lic[...])
    forward(3)
    for i in range(4, lag):
        forward(i)

    sends = []
    in_store = lambda peer: (peer, v)
    in_vocab = lambda peer: (s, peer)

    def share_row(row, slots, peers, index, send_sem, recv_sem, place):
        for j, peer in enumerate(peers):
            copy = remote(row, slots.at[index], send_sem.at[j], recv_sem.at[j], *place(peer))
            copy.start()
            sends.append(copy)
        slots[index] = row[...]

    def take_rows(slots, sources, peers, send_sem, recv_sem, place):
        for j, (source, peer) in enumerate(zip(sources, peers)):
            slot = slots.at[source]
            remote(slot, slot, send_sem.at[j], recv_sem.at[j], *place(peer)).wait_recv()

    def near_local(h):
        permitted = jnp.bitwise_and(
            jnp.right_shift(
                jnp.broadcast_to(allowed_row[h], (E, Q)), jnp.broadcast_to(turn[:, 0:1], (E, Q))
            ), 1) == 1
        masked = jnp.where(
            permitted, scores[h] * inverse_root - (0.5 * inverse_root) * half[:, 0:1], NEG_FILL
        )
        near = jnp.max(masked, axis=0, keepdims=True)
        kernel = jnp.where(permitted, jnp.exp(masked - near), 0.0)
        mass = jnp.sum(kernel, axis=0, keepdims=True)
        some = mass > 0.0
        safe = jnp.where(some, mass, 1.0)
        row_own[h, 1:2, :] = jnp.where(some, near + jnp.log(safe), NEG_FILL)
        wsend[h] = (kernel * (1.0 / safe)).astype(jnp.bfloat16)
        for j in range(1, V):
            peer = vocab_peers[j - 1]
            copy = remote(
                wsend.at[h, pl.ds(pl.multiple_of(peer * B, B), B)], wrecv.at[h, v],
                wsend_sem.at[h, j - 1], wrecv_sem.at[h, j - 1], s, peer,
            )
            copy.start()
            sends.append(copy)
        wrecv[h, v] = wsend[h, pl.ds(pl.multiple_of(v * B, B), B), :]

    def near_share(h, out, near_log, near_from):
        for j in range(1, V):
            slot = wrecv.at[h, vocab_from[j - 1]]
            remote(
                slot, slot, wsend_sem.at[h, j - 1], wrecv_sem.at[h, j - 1], s, vocab_peers[j - 1]
            ).wait_recv()
        for u in range(V):
            scale = jnp.exp(near_from(u) - near_log + (LIFT + math.log(0.25)))
            weights[u * B:(u + 1) * B, :] = (
                wrecv[h, u].astype(jnp.float32) * scale
            ).astype(jnp.bfloat16)
        out[...] = lax.dot_general(
            weights[...], table[...], (((0,), (0,)), ((), ())), preferred_element_type=jnp.float32
        ).reshape(S, RH, C)

    RT = math.gcd(Q, 128)
    G = RT // RH

    def lm_local(h):
        for r in range(0, Q, RT):
            tile = logits[h, r // RH:r // RH + G].reshape(RT, C)
            top = jnp.max(tile, axis=1, keepdims=True)
            total = jnp.sum(jnp.exp(tile - top), axis=1, keepdims=True)
            both = jnp.broadcast_to(top + jnp.log(total), (RT, 128))
            row_own[h, 0:1, r:r + RT] = both.T[0:1, :]

    def shift_from(lm_log):
        shift_out[...] = row_to_column(lm_log - math.log(0.75)).reshape(S, RH, 128)

    def first_round(h):
        share_row(row_own.at[h], row_all, store_peers, s, r1send, r1recv, in_store)

    def second_round(h):
        take_rows(row_all, store_from, store_peers, r1send, r1recv, in_store)
        row_mid[0:2, :] = log_sum_exp([row_all[i] for i in range(S)])
        row_mid[2:3, :] = row_own[h, 1:2, :]
        row_mid[3:4, :] = row_own[h, 1:2, :]
        share_row(row_mid, row_end, vocab_peers, v, r2send, r2recv, in_vocab)

    def two_rounds_end(h, out):
        take_rows(row_end, vocab_from, vocab_peers, r2send, r2recv, in_vocab)
        logs = log_sum_exp([row_end[u, 0:2, :] for u in range(V)])
        near_share(h, out, logs[1:2, :], lambda u: row_end[u, 2:3, :])
        shift_from(logs[0:1, :])

    steps = [(a, b) for b in reversed(range(V)) for a in reversed(range(S)) if a or b]

    def one_round(h):
        for j, (a, b) in enumerate(steps):
            copy = remote(
                row_own.at[h], row_every.at[s * V + v], esend.at[j], erecv.at[j],
                lax.rem(s + a, S), lax.rem(v + b, V),
            )
            copy.start()
            sends.append(copy)
        row_every[s * V + v] = row_own[h]

    def one_round_end(h, out):
        for j, (a, b) in enumerate(steps):
            slot = row_every.at[lax.rem(s + S - a, S) * V + lax.rem(v + V - b, V)]
            remote(
                slot, slot, esend.at[j], erecv.at[j], lax.rem(s + a, S), lax.rem(v + b, V)
            ).wait_recv()
        logs = log_sum_exp([row_every[i] for i in range(S * V)])
        near_share(h, out, logs[1:2, :], lambda u: row_every[s * V + u, 1:2, :])
        shift_from(logs[0:1, :])

    def early_mix():
        def tile(n, carry):
            span = pl.ds(n * G, G)
            logits[0, span] = mix(logits[0, span], share[span], shift_out[span, :, 0:1])
            return carry
        lax.fori_loop(0, S // G, tile, 0)

    last = H - 1
    if tuned:
        lax.fori_loop(lag, K + lag, gather_step, 0)
        near_local(0)
        lm_local(0)
        first_round(0)
        lax.fori_loop(K + lag, T - 1 + lag, gather_step, 0)
    else:
        lax.fori_loop(0, T - 1, gather_step, 0)
    last = H - 1
    ready(T - 1)
    add_scores(T - 1)
    near_local(last)
    add_logits(T - 1)
    if tuned:
        second_round(0)
        lm_local(last)
        one_round(last)
        two_rounds_end(0, share)
        early_mix()
        one_round_end(last, share_out)
    else:
        lm_local(last)
        first_round(last)
        second_round(last)
        two_rounds_end(last, share_out)

    for t in range(len(streams)):
        loop(T, lambda i: send(t, i).wait_send())
    for copy in token_sends + sends:
        copy.wait_send()


def mixture_kernel(logits, share, shift, out):
    G, H = out.shape[0], out.shape[1]
    span = pl.ds(pl.program_id(0) * G, G)
    for h in range(H - 1):
        out[:, h] = logits[h, span]
    out[:, H - 1] = mix(logits[H - 1, span], share[span], shift[span, :, 0:1])


def body(S, V, hidden, lm_head, keys, values, licences, allowed):
    R, D = hidden.shape
    C = lm_head.shape[1]
    E = keys.shape[0]
    Q = allowed.shape[0]
    B = E // V
    H = 2 if S == 8 and V % 2 == 0 and R % 32 == 0 else 1
    RH = R // H
    QH = Q // H
    KC = math.gcd(D, DEPTH_CHUNK)
    K = D // KC
    T = H * K
    streams = S - 1
    hbm = pl.BlockSpec(memory_space=pltpu.HBM)
    vmem = pl.BlockSpec(memory_space=pltpu.VMEM)
    f32 = jnp.float32
    bf16 = jnp.bfloat16
    dma = pltpu.SemaphoreType.DMA
    logits, share, shift = pl.pallas_call(
        functools.partial(gather_kernel, S, V),
        out_shape=(
            pltpu.VMEM((H, S, RH, C), f32), pltpu.VMEM((S, RH, C), f32), pltpu.VMEM((S, RH, 128), f32)
        ),
        in_specs=[hbm] * 6,
        out_specs=(vmem, vmem, vmem),
        scratch_shapes=[
            pltpu.VMEM((H, S, K, RH, KC), hidden.dtype),
            pltpu.VMEM((K, KC, C), lm_head.dtype),
            pltpu.VMEM((K, E, KC), keys.dtype),
            pltpu.VMEM((1, E), jnp.int32),
            pltpu.VMEM((1, Q), jnp.int32),
            pltpu.VMEM((1, E), jnp.int32),
            pltpu.VMEM((H, E, QH), f32),
            pltpu.VMEM((E, 128), f32),
            pltpu.VMEM((H, E, QH), bf16),
            pltpu.VMEM((H, V, B, QH), bf16),
            pltpu.VMEM((E, QH), bf16),
            pltpu.VMEM((S, RH, C), f32),
            pltpu.VMEM((E, C), bf16),
            pltpu.VMEM((8, E), jnp.int32),
            pltpu.VMEM((V, 8, E), jnp.int32),
            pltpu.VMEM((E, 128), jnp.int32),
            pltpu.VMEM((Q, 128), jnp.int32),
            pltpu.VMEM((H, 2, QH), f32),
            pltpu.VMEM((S, 2, QH), f32),
            pltpu.VMEM((4, QH), f32),
            pltpu.VMEM((V, 4, QH), f32),
            pltpu.VMEM((S * V, 2, QH) if H == 2 else (1, 2, QH), f32),
            dma((T,)), dma((K,)), dma((K,)), dma((3,)),
            dma((streams, T)), dma((streams, T)),
            dma((V - 1,)), dma((V - 1,)), dma((H, V - 1)), dma((H, V - 1)),
            dma((S - 1,)), dma((S - 1,)), dma((V - 1,)), dma((V - 1,)),
            dma((S * V - 1 if H == 2 else 1,)), dma((S * V - 1 if H == 2 else 1,)),
        ],
        compiler_params=pltpu.CompilerParams(
            collective_id=0, has_side_effects=True, vmem_limit_bytes=48 * 1024 * 1024
        ),
        name="gather_score",
    )(*[
        pltpu.with_memory_space_constraint(x, pltpu.HBM)
        for x in (hidden, lm_head, keys, values.reshape(1, E), licences.reshape(1, E), allowed.reshape(1, Q))
    ])

    G = max(1, math.gcd(Q, 128) // R)
    return pl.pallas_call(
        mixture_kernel,
        grid=(S // G,),
        out_shape=jax.ShapeDtypeStruct((S, H, RH, C), f32),
        in_specs=[vmem, vmem, vmem],
        out_specs=pl.BlockSpec((G, H, RH, C), lambda n: (n, 0, 0, 0)),
        compiler_params=pltpu.CompilerParams(vmem_limit_bytes=8 * 1024 * 1024),
        name="mixture",
    )(logits, share, shift).reshape(Q, C)


def solution(mesh):
    return jax.shard_map(
        functools.partial(body, mesh.shape["store"], mesh.shape["vocab"]),
        mesh=mesh,
        in_specs=(
            P("store", None),
            P(None, ("store", "vocab")),
            P(("store", "vocab"), None),
            P(("store", "vocab")),
            P(("store", "vocab")),
            P(),
        ),
        out_specs=P(None, ("store", "vocab")),
        check_vma=False,
    )
```

```python
import functools
import math

import jax
import jax.numpy as jnp
from jax import lax
from jax.experimental import pallas as pl
from jax.experimental.pallas import tpu as pltpu
from jax.sharding import PartitionSpec as P

NEG_FILL = -1e30
LIFT = 40.0
DEPTH_CHUNK = 1024
MESH = pl.DeviceIdType.MESH
HOP_LAG = 3
USE_LAG = 4
AHEAD = 4
DIRECT = 0


def row_to_column(row, lanes=128):
    return jnp.broadcast_to(row, (lanes, row.shape[1])).T


def log_sum_exp(rows):
    top = functools.reduce(jnp.maximum, rows)
    total = functools.reduce(jnp.add, [jnp.exp(row - top) for row in rows])
    return top + jnp.log(total)


def mix(logits, share, shift):
    ours = logits - shift
    both = jnp.log(jnp.exp(ours + LIFT) + share) - LIFT
    return jnp.where(share > 0.0, both, ours)


def gather_kernel(
    S, V,
    hidden, lm_head, keys, values, licences, allowed,
    logits, share_out, shift_out,
    hid, head, key, lic, allow, val, scores, half, wsend, wrecv, weights, share, table, tok, tokcol, turn, turned,
    row_own, row_all, row_mid, row_end, row_every,
    own_sem, head_sem, key_sem, small_sem, gsend, grecv, tsend, trecv, wsend_sem, wrecv_sem,
    r1send, r1recv, r2send, r2recv, esend, erecv,
):
    R, D = hidden.shape
    C = lm_head.shape[1]
    E = keys.shape[0]
    H, K, RH, KC = hid.shape[0], hid.shape[2], hid.shape[3], hid.shape[4]
    Q = S * RH
    T = H * K
    B = E // V
    inverse_root = 1.0 / math.sqrt(D)
    s = lax.axis_index("store")
    v = lax.axis_index("vocab")

    def depth(k):
        return pl.ds(pl.multiple_of(k * KC, KC), KC)

    def place_of(i):
        return lax.div(i, K), lax.rem(i, K)

    def remote(src, dst, send, recv, store, vocab):
        return pltpu.make_async_remote_copy(
            src_ref=src, dst_ref=dst, send_sem=send, recv_sem=recv,
            device_id=(store, vocab), device_id_type=MESH,
        )

    def own_rows(i):
        h, k = place_of(i)
        return hidden.at[pl.ds(pl.multiple_of(h * RH, RH), RH), depth(k)]

    def block(i, origin):
        h, k = place_of(i)
        return hid.at[h, origin, k]

    def own_copy(i):
        return pltpu.make_async_copy(own_rows(i), block(i, s), own_sem.at[i])

    def head_copy(k):
        return pltpu.make_async_copy(lm_head.at[depth(k)], head.at[k], head_sem.at[k])

    def key_copy(k):
        return pltpu.make_async_copy(keys.at[:, depth(k)], key.at[k], key_sem.at[k])

    def loop(n, f):
        def step(k, carry):
            f(k)
            return carry
        lax.fori_loop(0, n, step, 0)

    store_peers = [lax.rem(s + j, S) for j in range(1, S)]
    vocab_peers = [lax.rem(v + j, V) for j in range(1, V)]
    vocab_from = [lax.rem(v + V - j, V) for j in range(1, V)]
    store_from = [lax.rem(s + S - j, S) for j in range(1, S)]

    barrier = pltpu.get_barrier_semaphore()
    for peer in store_peers:
        pl.semaphore_signal(barrier, inc=1, device_id=(peer, v), device_id_type=MESH)
    for peer in vocab_peers:
        pl.semaphore_signal(barrier, inc=1, device_id=(s, peer), device_id_type=MESH)

    small = [
        pltpu.make_async_copy(src, dst, small_sem.at[i])
        for i, (src, dst) in enumerate(((values, val), (licences, lic), (allowed, allow)))
    ]
    for copy in small:
        copy.start()
    loop(K, lambda k: key_copy(k).start())
    loop(T, lambda i: own_copy(i).start())

    pl.semaphore_wait(barrier, S + V - 2)

    tuned = H == 2
    if tuned:
        odd = lax.rem(v, 2)
        along_x = 2 - 4 * lax.rem(lax.div(s, 2), 2)
        along_y = 4 - 8 * lax.rem(lax.div(s, 4), 2)
        across = 1 - 2 * lax.rem(s, 2)
        pair = v + 1 - 2 * odd
        diagonal = s + along_x + along_y

    def direct(i):
        return i >= T - DIRECT

    def stream(t, i):
        if not tuned:
            return s, (store_peers[t], v), store_from[t]
        turn_i = lax.rem(odd + i, 2)
        first = s + along_x * (1 - turn_i) + along_y * turn_i
        second = s + along_y * (1 - turn_i) + along_x * turn_i
        return (
            (s, (first, v), first),
            (first, (second, v), diagonal),
            (first, (s, pair), second),
            (s, (s + across, v), s + across),
            (first, (s + across, v), first + across),
            (diagonal, (s + across, v), diagonal + across),
            (second, (s + across, v), second + across),
            (s, (second, v), second),
        )[t]

    def send(t, i):
        origin, target, _ = stream(t, i)
        own = not tuned or t in (0, 3, 7)
        src = own_rows(i) if own else block(i, origin)
        t = 2 if t == 7 else t
        return remote(src, block(i, origin), gsend.at[t, i], grecv.at[t, i], *target)

    def arrive(t, i):
        _, target, origin = stream(t, i)
        return remote(block(i, origin), block(i, origin), gsend.at[t, i], grecv.at[t, i], *target)

    def begin(i):
        send(0, i).start()
        @pl.when(direct(i))
        def _():
            send(7, i).start()

    if tuned:
        loop(AHEAD, begin)
        loop(T, lambda i: send(3, i).start())
    else:
        for t in range(S - 1):
            loop(T, lambda i: send(t, i).start())
    loop(K, lambda k: head_copy(k).start())

    for copy in small:
        copy.wait()
    tok[...] = jnp.broadcast_to(val[...], tok.shape)
    token_sends = []
    for j in range(1, V):
        copy = remote(tok, tokcol.at[v], tsend.at[j - 1], trecv.at[j - 1], s, vocab_peers[j - 1])
        copy.start()
        token_sends.append(copy)
    tokcol[v] = tok[...]

    def forward(i):
        if not tuned:
            return
        @pl.when(i < T)
        def _():
            arrive(0, i).wait_recv()
            send(1, i).start()
            @pl.when(jnp.logical_not(direct(i)))
            def _():
                send(2, i).start()
            send(4, i).start()
            @pl.when(i + AHEAD < T)
            def _():
                begin(i + AHEAD)

        @pl.when(jnp.logical_and(i >= HOP_LAG, i < T + HOP_LAG))
        def _():
            arrive(1, i - HOP_LAG).wait_recv()
            send(5, i - HOP_LAG).start()
            arrive(2, i - HOP_LAG).wait_recv()
            send(6, i - HOP_LAG).start()

    lag = USE_LAG if tuned else 0

    def ready(i):
        if not tuned:
            @pl.when(i < K)
            def _():
                head_copy(i).wait()
            own_copy(i).wait()
        for t in range(4, 7) if tuned else range(S - 1):
            arrive(t, i).wait_recv()

    chip = lax.div(s, 2)
    around = [lax.rem(chip + j, S // 2) for j in range(S // 2)]

    def early_logits(k):
        head_copy(k).wait()
        for i in (k, K + k):
            own_copy(i).wait()
            arrive(3, i).wait_recv()
        own = pl.ds(2 * chip, 2)
        both = jnp.concatenate([hid[h, own, k].reshape(2 * RH, KC) for h in range(H)], axis=0)
        part = jnp.dot(both, head[k], preferred_element_type=jnp.float32)
        for h in range(H):
            logits[h, own] += part[2 * h * RH:2 * (h + 1) * RH].reshape(2, RH, C)

    def states(i):
        h, k = place_of(i)
        return hid[h, :, k].reshape(Q, KC)

    def add_scores(i):
        h, k = place_of(i)
        scores[h] += lax.dot_general(
            key[k], states(i), (((1,), (1,)), ((), ())), preferred_element_type=jnp.float32
        )

    def add_logits(i):
        h, k = place_of(i)
        if tuned:
            others = [pl.ds(2 * chip_of, 2) for chip_of in around[1:]]
        else:
            others = [pl.ds(0, S)]
        rows = S * RH // (S // 2 if tuned else 1)
        lhs = jnp.concatenate([hid[h, other, k].reshape(rows, KC) for other in others], axis=0)
        part = jnp.dot(lhs, head[k], preferred_element_type=jnp.float32)
        for j, other in enumerate(others):
            piece = part[j * rows:(j + 1) * rows]
            logits[h, other] += piece.reshape(rows // RH, RH, C)

    def norm_step(k):
        key_copy(k).wait()
        wide = key[k].astype(jnp.float32)
        square = wide * wide
        half[...] += functools.reduce(
            jnp.add, [square[:, i:i + 128] for i in range(0, KC, 128)]
        )

    def gather_step(i, carry):
        forward(i)
        ready(i - lag)
        add_scores(i - lag)
        add_logits(i - lag)
        return carry

    first_col = (s * V + v) * C
    half[...] = jnp.zeros_like(half)
    scores[...] = jnp.zeros_like(scores)
    logits[...] = jnp.zeros_like(logits)
    loop(K, norm_step)
    turned[...] = row_to_column(allow[...])
    half[...] = jnp.broadcast_to(jnp.sum(half[...], axis=1, keepdims=True), half.shape)
    allowed_row = [
        jnp.concatenate(
            [turned[o * R + h * RH:o * R + (h + 1) * RH, :] for o in range(S)], axis=0
        ).T[0:1, :]
        for h in range(H)
    ]

    def fill(i, carry):
        forward(i)
        early_logits(i)
        return carry

    if tuned:
        lax.fori_loop(0, K, fill, 0)
        for i in range(K, lag):
            forward(i)
    for j in range(1, V):
        slot = tokcol.at[vocab_from[j - 1]]
        remote(slot, slot, tsend.at[j - 1], trecv.at[j - 1], s, vocab_peers[j - 1]).wait_recv()
    for u in range(V):
        turn[...] = row_to_column(tokcol[u, 0:1, :])
        mine = turn[pl.ds(pl.multiple_of(v * B, B), B), 0:1] - first_col
        columns = lax.broadcasted_iota(jnp.int32, (B, C), 1)
        table[u * B:(u + 1) * B, :] = jnp.where(mine == columns, 1.0, 0.0).astype(jnp.bfloat16)
    turn[...] = row_to_column(lic[...])

    sends = []
    in_store = lambda peer: (peer, v)
    in_vocab = lambda peer: (s, peer)

    def share_row(row, slots, peers, index, send_sem, recv_sem, place):
        for j, peer in enumerate(peers):
            copy = remote(row, slots.at[index], send_sem.at[j], recv_sem.at[j], *place(peer))
            copy.start()
            sends.append(copy)
        slots[index] = row[...]

    def take_rows(slots, sources, peers, send_sem, recv_sem, place):
        for j, (source, peer) in enumerate(zip(sources, peers)):
            slot = slots.at[source]
            remote(slot, slot, send_sem.at[j], recv_sem.at[j], *place(peer)).wait_recv()

    def near_local(h):
        permitted = jnp.bitwise_and(
            jnp.right_shift(
                jnp.broadcast_to(allowed_row[h], (E, Q)), jnp.broadcast_to(turn[:, 0:1], (E, Q))
            ), 1) == 1
        masked = jnp.where(
            permitted, scores[h] * inverse_root - (0.5 * inverse_root) * half[:, 0:1], NEG_FILL
        )
        near = jnp.max(masked, axis=0, keepdims=True)
        kernel = jnp.where(permitted, jnp.exp(masked - near), 0.0)
        mass = jnp.sum(kernel, axis=0, keepdims=True)
        some = mass > 0.0
        safe = jnp.where(some, mass, 1.0)
        row_own[h, 1:2, :] = jnp.where(some, near + jnp.log(safe), NEG_FILL)
        wsend[h] = (kernel * (1.0 / safe)).astype(jnp.bfloat16)
        for j in range(1, V):
            peer = vocab_peers[j - 1]
            copy = remote(
                wsend.at[h, pl.ds(pl.multiple_of(peer * B, B), B)], wrecv.at[h, v],
                wsend_sem.at[h, j - 1], wrecv_sem.at[h, j - 1], s, peer,
            )
            copy.start()
            sends.append(copy)
        wrecv[h, v] = wsend[h, pl.ds(pl.multiple_of(v * B, B), B), :]

    def near_share(h, out, near_log, near_from):
        for j in range(1, V):
            slot = wrecv.at[h, vocab_from[j - 1]]
            remote(
                slot, slot, wsend_sem.at[h, j - 1], wrecv_sem.at[h, j - 1], s, vocab_peers[j - 1]
            ).wait_recv()
        for u in range(V):
            scale = jnp.exp(near_from(u) - near_log + (LIFT + math.log(0.25)))
            weights[u * B:(u + 1) * B, :] = (
                wrecv[h, u].astype(jnp.float32) * scale
            ).astype(jnp.bfloat16)
        out[...] = lax.dot_general(
            weights[...], table[...], (((0,), (0,)), ((), ())), preferred_element_type=jnp.float32
        ).reshape(S, RH, C)

    RT = math.gcd(Q, 128)
    G = RT // RH

    def lm_local(h):
        for r in range(0, Q, RT):
            tile = logits[h, r // RH:r // RH + G].reshape(RT, C)
            top = jnp.max(tile, axis=1, keepdims=True)
            total = jnp.sum(jnp.exp(tile - top), axis=1, keepdims=True)
            both = jnp.broadcast_to(top + jnp.log(total), (RT, 128))
            row_own[h, 0:1, r:r + RT] = both.T[0:1, :]

    def shift_from(lm_log):
        shift_out[...] = row_to_column(lm_log - math.log(0.75)).reshape(S, RH, 128)

    def first_round(h):
        share_row(row_own.at[h], row_all, store_peers, s, r1send, r1recv, in_store)

    def second_round(h):
        take_rows(row_all, store_from, store_peers, r1send, r1recv, in_store)
        row_mid[0:2, :] = log_sum_exp([row_all[i] for i in range(S)])
        row_mid[2:3, :] = row_own[h, 1:2, :]
        row_mid[3:4, :] = row_own[h, 1:2, :]
        share_row(row_mid, row_end, vocab_peers, v, r2send, r2recv, in_vocab)

    def two_rounds_end(h, out):
        take_rows(row_end, vocab_from, vocab_peers, r2send, r2recv, in_vocab)
        logs = log_sum_exp([row_end[u, 0:2, :] for u in range(V)])
        near_share(h, out, logs[1:2, :], lambda u: row_end[u, 2:3, :])
        shift_from(logs[0:1, :])

    steps = [(a, b) for b in reversed(range(V)) for a in reversed(range(S)) if a or b]

    def one_round(h):
        for j, (a, b) in enumerate(steps):
            copy = remote(
                row_own.at[h], row_every.at[s * V + v], esend.at[j], erecv.at[j],
                lax.rem(s + a, S), lax.rem(v + b, V),
            )
            copy.start()
            sends.append(copy)
        row_every[s * V + v] = row_own[h]

    def one_round_end(h, out):
        for j, (a, b) in enumerate(steps):
            slot = row_every.at[lax.rem(s + S - a, S) * V + lax.rem(v + V - b, V)]
            remote(
                slot, slot, esend.at[j], erecv.at[j], lax.rem(s + a, S), lax.rem(v + b, V)
            ).wait_recv()
        logs = log_sum_exp([row_every[i] for i in range(S * V)])
        near_share(h, out, logs[1:2, :], lambda u: row_every[s * V + u, 1:2, :])
        shift_from(logs[0:1, :])

    def early_mix():
        def tile(n, carry):
            span = pl.ds(n * G, G)
            logits[0, span] = mix(logits[0, span], share[span], shift_out[span, :, 0:1])
            return carry
        lax.fori_loop(0, S // G, tile, 0)

    last = H - 1
    def drain():
        def wait_all(i):
            for t in range(S - 1):
                send(t, i).wait_send()
        loop(T, wait_all)

    if tuned:
        lax.fori_loop(lag, K + lag, gather_step, 0)
        near_local(0)
        lm_local(0)
        first_round(0)
        lax.fori_loop(K + lag, T - 1 + lag, gather_step, 0)
    else:
        lax.fori_loop(0, T - 1, gather_step, 0)
    last = H - 1
    if tuned:
        second_round(0)
    ready(T - 1)
    add_scores(T - 1)
    near_local(last)
    add_logits(T - 1)
    if tuned:
        lm_local(last)
        one_round(last)
        two_rounds_end(0, share)
        early_mix()
        drain()
        one_round_end(last, share_out)
    else:
        lm_local(last)
        first_round(last)
        second_round(last)
        two_rounds_end(last, share_out)

    if not tuned:
        drain()
    for copy in token_sends + sends:
        copy.wait_send()


def mixture_kernel(logits, share, shift, out, last, early_sem, late_sem):
    H, S, RH = logits.shape[:3]
    G = max(1, 64 // RH)
    early = [
        pltpu.make_async_copy(logits.at[h, o], out.at[o, h], early_sem.at[h, o])
        for h in range(H - 1) for o in range(S)
    ]
    for copy in early:
        copy.start()

    def late_copy(n):
        span = pl.ds(n * G, G)
        return pltpu.make_async_copy(last.at[span], out.at[span, H - 1], late_sem.at[n])

    def tile(n, carry):
        span = pl.ds(n * G, G)
        last[span] = mix(logits[H - 1, span], share[span], shift[span, :, 0:1])
        late_copy(n).start()
        return carry

    def finish(n, carry):
        late_copy(n).wait()
        return carry

    lax.fori_loop(0, S // G, tile, 0)
    for copy in early:
        copy.wait()
    lax.fori_loop(0, S // G, finish, 0)


def body(S, V, hidden, lm_head, keys, values, licences, allowed):
    R, D = hidden.shape
    C = lm_head.shape[1]
    E = keys.shape[0]
    Q = allowed.shape[0]
    B = E // V
    H = 2 if S == 8 and V % 2 == 0 and R % 32 == 0 else 1
    RH = R // H
    QH = Q // H
    KC = math.gcd(D, DEPTH_CHUNK)
    K = D // KC
    T = H * K
    streams = S - 1
    hbm = pl.BlockSpec(memory_space=pltpu.HBM)
    vmem = pl.BlockSpec(memory_space=pltpu.VMEM)
    f32 = jnp.float32
    bf16 = jnp.bfloat16
    dma = pltpu.SemaphoreType.DMA
    logits, share, shift = pl.pallas_call(
        functools.partial(gather_kernel, S, V),
        out_shape=(
            pltpu.VMEM((H, S, RH, C), f32), pltpu.VMEM((S, RH, C), f32), pltpu.VMEM((S, RH, 128), f32)
        ),
        in_specs=[hbm] * 6,
        out_specs=(vmem, vmem, vmem),
        scratch_shapes=[
            pltpu.VMEM((H, S, K, RH, KC), hidden.dtype),
            pltpu.VMEM((K, KC, C), lm_head.dtype),
            pltpu.VMEM((K, E, KC), keys.dtype),
            pltpu.VMEM((1, E), jnp.int32),
            pltpu.VMEM((1, Q), jnp.int32),
            pltpu.VMEM((1, E), jnp.int32),
            pltpu.VMEM((H, E, QH), f32),
            pltpu.VMEM((E, 128), f32),
            pltpu.VMEM((H, E, QH), bf16),
            pltpu.VMEM((H, V, B, QH), bf16),
            pltpu.VMEM((E, QH), bf16),
            pltpu.VMEM((S, RH, C), f32),
            pltpu.VMEM((E, C), bf16),
            pltpu.VMEM((8, E), jnp.int32),
            pltpu.VMEM((V, 8, E), jnp.int32),
            pltpu.VMEM((E, 128), jnp.int32),
            pltpu.VMEM((Q, 128), jnp.int32),
            pltpu.VMEM((H, 2, QH), f32),
            pltpu.VMEM((S, 2, QH), f32),
            pltpu.VMEM((4, QH), f32),
            pltpu.VMEM((V, 4, QH), f32),
            pltpu.VMEM((S * V, 2, QH) if H == 2 else (1, 2, QH), f32),
            dma((T,)), dma((K,)), dma((K,)), dma((3,)),
            dma((streams, T)), dma((streams, T)),
            dma((V - 1,)), dma((V - 1,)), dma((H, V - 1)), dma((H, V - 1)),
            dma((S - 1,)), dma((S - 1,)), dma((V - 1,)), dma((V - 1,)),
            dma((S * V - 1 if H == 2 else 1,)), dma((S * V - 1 if H == 2 else 1,)),
        ],
        compiler_params=pltpu.CompilerParams(
            collective_id=0, has_side_effects=True, vmem_limit_bytes=48 * 1024 * 1024
        ),
        name="gather_score",
    )(*[
        pltpu.with_memory_space_constraint(x, pltpu.HBM)
        for x in (hidden, lm_head, keys, values.reshape(1, E), licences.reshape(1, E), allowed.reshape(1, Q))
    ])

    return pl.pallas_call(
        mixture_kernel,
        out_shape=jax.ShapeDtypeStruct((S, H, RH, C), f32),
        in_specs=[vmem, vmem, vmem],
        out_specs=hbm,
        scratch_shapes=[pltpu.VMEM((S, RH, C), f32), dma((H, S)), dma((S,))],
        compiler_params=pltpu.CompilerParams(vmem_limit_bytes=8 * 1024 * 1024),
        name="mixture",
    )(logits, share, shift).reshape(Q, C)


def solution(mesh):
    return jax.shard_map(
        functools.partial(body, mesh.shape["store"], mesh.shape["vocab"]),
        mesh=mesh,
        in_specs=(
            P("store", None),
            P(None, ("store", "vocab")),
            P(("store", "vocab"), None),
            P(("store", "vocab")),
            P(("store", "vocab")),
            P(),
        ),
        out_specs=P(None, ("store", "vocab")),
        check_vma=False,
    )
```

```python
import functools
import math

import jax
import jax.numpy as jnp
from jax import lax
from jax.experimental import pallas as pl
from jax.experimental.pallas import tpu as pltpu
from jax.sharding import PartitionSpec as P

NEG_FILL = -1e30
LIFT = 40.0
DEPTH_CHUNK = 1024
MESH = pl.DeviceIdType.MESH
HOP_LAG = 3
USE_LAG = 4
AHEAD = 4
DIRECT = 0


def row_to_column(row, lanes=128):
    return jnp.broadcast_to(row, (lanes, row.shape[1])).T


def log_sum_exp(rows):
    top = functools.reduce(jnp.maximum, rows)
    total = functools.reduce(jnp.add, [jnp.exp(row - top) for row in rows])
    return top + jnp.log(total)


def mix(logits, share, shift):
    ours = logits - shift
    both = jnp.log(jnp.exp(ours + LIFT) + share) - LIFT
    return jnp.where(share > 0.0, both, ours)


def gather_kernel(
    S, V,
    hidden, lm_head, keys, values, licences, allowed,
    logits, share_out, shift_out,
    hid, head, key, lic, allow, val, scores, half, wsend, wrecv, weights, share, table, tok, tokcol, turn, turned,
    row_own, row_all, row_mid, row_end, row_every, lm_row, near_row, near_all, near_mid, near_end,
    own_sem, head_sem, key_sem, small_sem, gsend, grecv, tsend, trecv, wsend_sem, wrecv_sem,
    r1send, r1recv, r2send, r2recv, esend, erecv, n1send, n1recv, n2send, n2recv,
):
    R, D = hidden.shape
    C = lm_head.shape[1]
    E = keys.shape[0]
    H, K, RH, KC = hid.shape[0], hid.shape[2], hid.shape[3], hid.shape[4]
    Q = S * RH
    T = H * K
    B = E // V
    inverse_root = 1.0 / math.sqrt(D)
    s = lax.axis_index("store")
    v = lax.axis_index("vocab")

    def depth(k):
        return pl.ds(pl.multiple_of(k * KC, KC), KC)

    def place_of(i):
        return lax.div(i, K), lax.rem(i, K)

    def remote(src, dst, send, recv, store, vocab):
        return pltpu.make_async_remote_copy(
            src_ref=src, dst_ref=dst, send_sem=send, recv_sem=recv,
            device_id=(store, vocab), device_id_type=MESH,
        )

    def own_rows(i):
        h, k = place_of(i)
        return hidden.at[pl.ds(pl.multiple_of(h * RH, RH), RH), depth(k)]

    def block(i, origin):
        h, k = place_of(i)
        return hid.at[h, origin, k]

    def own_copy(i):
        return pltpu.make_async_copy(own_rows(i), block(i, s), own_sem.at[i])

    def head_copy(k):
        return pltpu.make_async_copy(lm_head.at[depth(k)], head.at[k], head_sem.at[k])

    def key_copy(k):
        return pltpu.make_async_copy(keys.at[:, depth(k)], key.at[k], key_sem.at[k])

    def loop(n, f):
        def step(k, carry):
            f(k)
            return carry
        lax.fori_loop(0, n, step, 0)

    store_peers = [lax.rem(s + j, S) for j in range(1, S)]
    vocab_peers = [lax.rem(v + j, V) for j in range(1, V)]
    vocab_from = [lax.rem(v + V - j, V) for j in range(1, V)]
    store_from = [lax.rem(s + S - j, S) for j in range(1, S)]

    barrier = pltpu.get_barrier_semaphore()
    for peer in store_peers:
        pl.semaphore_signal(barrier, inc=1, device_id=(peer, v), device_id_type=MESH)
    for peer in vocab_peers:
        pl.semaphore_signal(barrier, inc=1, device_id=(s, peer), device_id_type=MESH)

    small = [
        pltpu.make_async_copy(src, dst, small_sem.at[i])
        for i, (src, dst) in enumerate(((values, val), (licences, lic), (allowed, allow)))
    ]
    for copy in small:
        copy.start()
    loop(K, lambda k: key_copy(k).start())
    loop(T, lambda i: own_copy(i).start())

    pl.semaphore_wait(barrier, S + V - 2)

    tuned = H == 2
    if tuned:
        odd = lax.rem(v, 2)
        along_x = 2 - 4 * lax.rem(lax.div(s, 2), 2)
        along_y = 4 - 8 * lax.rem(lax.div(s, 4), 2)
        across = 1 - 2 * lax.rem(s, 2)
        pair = v + 1 - 2 * odd
        diagonal = s + along_x + along_y

    def direct(i):
        return i >= T - DIRECT

    def stream(t, i):
        if not tuned:
            return s, (store_peers[t], v), store_from[t]
        turn_i = lax.rem(odd + i, 2)
        first = s + along_x * (1 - turn_i) + along_y * turn_i
        second = s + along_y * (1 - turn_i) + along_x * turn_i
        return (
            (s, (first, v), first),
            (first, (second, v), diagonal),
            (first, (s, pair), second),
            (s, (s + across, v), s + across),
            (first, (s + across, v), first + across),
            (diagonal, (s + across, v), diagonal + across),
            (second, (s + across, v), second + across),
            (s, (second, v), second),
        )[t]

    def send(t, i):
        origin, target, _ = stream(t, i)
        own = not tuned or t in (0, 3, 7)
        src = own_rows(i) if own else block(i, origin)
        t = 2 if t == 7 else t
        return remote(src, block(i, origin), gsend.at[t, i], grecv.at[t, i], *target)

    def arrive(t, i):
        _, target, origin = stream(t, i)
        return remote(block(i, origin), block(i, origin), gsend.at[t, i], grecv.at[t, i], *target)

    def begin(i):
        send(0, i).start()
        @pl.when(direct(i))
        def _():
            send(7, i).start()

    if tuned:
        loop(AHEAD, begin)
        loop(T, lambda i: send(3, i).start())
    else:
        for t in range(S - 1):
            loop(T, lambda i: send(t, i).start())
    loop(K, lambda k: head_copy(k).start())

    for copy in small:
        copy.wait()
    tok[...] = jnp.broadcast_to(val[...], tok.shape)
    token_sends = []
    for j in range(1, V):
        copy = remote(tok, tokcol.at[v], tsend.at[j - 1], trecv.at[j - 1], s, vocab_peers[j - 1])
        copy.start()
        token_sends.append(copy)
    tokcol[v] = tok[...]

    def forward(i):
        if not tuned:
            return
        @pl.when(i < T)
        def _():
            arrive(0, i).wait_recv()
            send(1, i).start()
            @pl.when(jnp.logical_not(direct(i)))
            def _():
                send(2, i).start()
            send(4, i).start()
            @pl.when(i + AHEAD < T)
            def _():
                begin(i + AHEAD)

        @pl.when(jnp.logical_and(i >= HOP_LAG, i < T + HOP_LAG))
        def _():
            arrive(1, i - HOP_LAG).wait_recv()
            send(5, i - HOP_LAG).start()
            arrive(2, i - HOP_LAG).wait_recv()
            send(6, i - HOP_LAG).start()

    lag = USE_LAG if tuned else 0

    def ready(i):
        if not tuned:
            @pl.when(i < K)
            def _():
                head_copy(i).wait()
            own_copy(i).wait()
        for t in range(4, 7) if tuned else range(S - 1):
            arrive(t, i).wait_recv()

    chip = lax.div(s, 2)
    around = [lax.rem(chip + j, S // 2) for j in range(S // 2)]

    def early_logits(k):
        head_copy(k).wait()
        for i in (k, K + k):
            own_copy(i).wait()
            arrive(3, i).wait_recv()
        own = pl.ds(2 * chip, 2)
        both = jnp.concatenate([hid[h, own, k].reshape(2 * RH, KC) for h in range(H)], axis=0)
        part = jnp.dot(both, head[k], preferred_element_type=jnp.float32)
        for h in range(H):
            logits[h, own] += part[2 * h * RH:2 * (h + 1) * RH].reshape(2, RH, C)

    def states(i):
        h, k = place_of(i)
        return hid[h, :, k].reshape(Q, KC)

    def add_scores(i):
        h, k = place_of(i)
        scores[h] += lax.dot_general(
            key[k], states(i), (((1,), (1,)), ((), ())), preferred_element_type=jnp.float32
        )

    def add_logits(i):
        h, k = place_of(i)
        if tuned:
            others = [pl.ds(2 * chip_of, 2) for chip_of in around[1:]]
        else:
            others = [pl.ds(0, S)]
        rows = S * RH // (S // 2 if tuned else 1)
        lhs = jnp.concatenate([hid[h, other, k].reshape(rows, KC) for other in others], axis=0)
        part = jnp.dot(lhs, head[k], preferred_element_type=jnp.float32)
        for j, other in enumerate(others):
            piece = part[j * rows:(j + 1) * rows]
            logits[h, other] += piece.reshape(rows // RH, RH, C)

    def norm_step(k):
        key_copy(k).wait()
        wide = key[k].astype(jnp.float32)
        square = wide * wide
        half[...] += functools.reduce(
            jnp.add, [square[:, i:i + 128] for i in range(0, KC, 128)]
        )

    def gather_step(i, carry):
        forward(i)
        ready(i - lag)
        add_scores(i - lag)
        add_logits(i - lag)
        return carry

    first_col = (s * V + v) * C
    half[...] = jnp.zeros_like(half)
    scores[...] = jnp.zeros_like(scores)
    logits[...] = jnp.zeros_like(logits)
    loop(K, norm_step)
    turned[...] = row_to_column(allow[...])
    half[...] = jnp.broadcast_to(jnp.sum(half[...], axis=1, keepdims=True), half.shape)
    allowed_row = [
        jnp.concatenate(
            [turned[o * R + h * RH:o * R + (h + 1) * RH, :] for o in range(S)], axis=0
        ).T[0:1, :]
        for h in range(H)
    ]

    def fill(i, carry):
        forward(i)
        early_logits(i)
        return carry

    if tuned:
        lax.fori_loop(0, K, fill, 0)
        for i in range(K, lag):
            forward(i)
    for j in range(1, V):
        slot = tokcol.at[vocab_from[j - 1]]
        remote(slot, slot, tsend.at[j - 1], trecv.at[j - 1], s, vocab_peers[j - 1]).wait_recv()
    for u in range(V):
        turn[...] = row_to_column(tokcol[u, 0:1, :])
        mine = turn[pl.ds(pl.multiple_of(v * B, B), B), 0:1] - first_col
        columns = lax.broadcasted_iota(jnp.int32, (B, C), 1)
        table[u * B:(u + 1) * B, :] = jnp.where(mine == columns, 1.0, 0.0).astype(jnp.bfloat16)
    turn[...] = row_to_column(lic[...])

    sends = []
    in_store = lambda peer: (peer, v)
    in_vocab = lambda peer: (s, peer)

    def share_row(row, slots, peers, index, send_sem, recv_sem, place):
        for j, peer in enumerate(peers):
            copy = remote(row, slots.at[index], send_sem.at[j], recv_sem.at[j], *place(peer))
            copy.start()
            sends.append(copy)
        slots[index] = row[...]

    def take_rows(slots, sources, peers, send_sem, recv_sem, place):
        for j, (source, peer) in enumerate(zip(sources, peers)):
            slot = slots.at[source]
            remote(slot, slot, send_sem.at[j], recv_sem.at[j], *place(peer)).wait_recv()

    def near_local(h, announce=lambda: None):
        permitted = jnp.bitwise_and(
            jnp.right_shift(
                jnp.broadcast_to(allowed_row[h], (E, Q)), jnp.broadcast_to(turn[:, 0:1], (E, Q))
            ), 1) == 1
        masked = jnp.where(
            permitted, scores[h] * inverse_root - (0.5 * inverse_root) * half[:, 0:1], NEG_FILL
        )
        near = jnp.max(masked, axis=0, keepdims=True)
        kernel = jnp.where(permitted, jnp.exp(masked - near), 0.0)
        mass = jnp.sum(kernel, axis=0, keepdims=True)
        some = mass > 0.0
        safe = jnp.where(some, mass, 1.0)
        row_own[h, 1:2, :] = jnp.where(some, near + jnp.log(safe), NEG_FILL)
        wsend[h] = (kernel * (1.0 / safe)).astype(jnp.bfloat16)
        announce()
        for j in range(1, V):
            peer = vocab_peers[j - 1]
            copy = remote(
                wsend.at[h, pl.ds(pl.multiple_of(peer * B, B), B)], wrecv.at[h, v],
                wsend_sem.at[h, j - 1], wrecv_sem.at[h, j - 1], s, peer,
            )
            copy.start()
            sends.append(copy)
        wrecv[h, v] = wsend[h, pl.ds(pl.multiple_of(v * B, B), B), :]

    def near_share(h, out, near_log, near_from):
        for j in range(1, V):
            slot = wrecv.at[h, vocab_from[j - 1]]
            remote(
                slot, slot, wsend_sem.at[h, j - 1], wrecv_sem.at[h, j - 1], s, vocab_peers[j - 1]
            ).wait_recv()
        for u in range(V):
            scale = jnp.exp(near_from(u) - near_log + (LIFT + math.log(0.25)))
            weights[u * B:(u + 1) * B, :] = (
                wrecv[h, u].astype(jnp.float32) * scale
            ).astype(jnp.bfloat16)
        out[...] = lax.dot_general(
            weights[...], table[...], (((0,), (0,)), ((), ())), preferred_element_type=jnp.float32
        ).reshape(S, RH, C)

    RT = math.gcd(Q, 128)
    G = RT // RH

    def lm_local(h):
        for r in range(0, Q, RT):
            tile = logits[h, r // RH:r // RH + G].reshape(RT, C)
            top = jnp.max(tile, axis=1, keepdims=True)
            total = jnp.sum(jnp.exp(tile - top), axis=1, keepdims=True)
            both = jnp.broadcast_to(top + jnp.log(total), (RT, 128))
            row_own[h, 0:1, r:r + RT] = both.T[0:1, :]

    def shift_from(lm_log):
        shift_out[...] = row_to_column(lm_log - math.log(0.75)).reshape(S, RH, 128)

    def first_round(h):
        share_row(row_own.at[h], row_all, store_peers, s, r1send, r1recv, in_store)

    def second_round(h):
        take_rows(row_all, store_from, store_peers, r1send, r1recv, in_store)
        row_mid[0:2, :] = log_sum_exp([row_all[i] for i in range(S)])
        row_mid[2:3, :] = row_own[h, 1:2, :]
        row_mid[3:4, :] = row_own[h, 1:2, :]
        share_row(row_mid, row_end, vocab_peers, v, r2send, r2recv, in_vocab)

    def two_rounds_end(h, out):
        take_rows(row_end, vocab_from, vocab_peers, r2send, r2recv, in_vocab)
        logs = log_sum_exp([row_end[u, 0:2, :] for u in range(V)])
        near_share(h, out, logs[1:2, :], lambda u: row_end[u, 2:3, :])
        shift_from(logs[0:1, :])

    steps = [(a, b) for b in reversed(range(V)) for a in reversed(range(S)) if a or b]

    def one_round(h):
        lm_row[...] = row_own[h, 0:1, :]
        for j, (a, b) in enumerate(steps):
            copy = remote(
                lm_row, row_every.at[s * V + v], esend.at[j], erecv.at[j],
                lax.rem(s + a, S), lax.rem(v + b, V),
            )
            copy.start()
            sends.append(copy)
        row_every[s * V + v] = lm_row[...]

    def near_first(h):
        near_row[...] = row_own[h, 1:2, :]
        share_row(near_row, near_all, store_peers, s, n1send, n1recv, in_store)

    def near_second():
        take_rows(near_all, store_from, store_peers, n1send, n1recv, in_store)
        near_mid[0:1, :] = log_sum_exp([near_all[i] for i in range(S)])
        near_mid[1:2, :] = near_row[...]
        share_row(near_mid, near_end, vocab_peers, v, n2send, n2recv, in_vocab)

    def one_round_end(h, out):
        take_rows(near_end, vocab_from, vocab_peers, n2send, n2recv, in_vocab)
        near_log = log_sum_exp([near_end[u, 0:1, :] for u in range(V)])
        near_share(h, out, near_log, lambda u: near_end[u, 1:2, :])
        for j, (a, b) in enumerate(steps):
            slot = row_every.at[lax.rem(s + S - a, S) * V + lax.rem(v + V - b, V)]
            remote(
                slot, slot, esend.at[j], erecv.at[j], lax.rem(s + a, S), lax.rem(v + b, V)
            ).wait_recv()
        shift_from(log_sum_exp([row_every[i] for i in range(S * V)]))

    def early_mix():
        def tile(n, carry):
            span = pl.ds(n * G, G)
            logits[0, span] = mix(logits[0, span], share[span], shift_out[span, :, 0:1])
            return carry
        lax.fori_loop(0, S // G, tile, 0)

    last = H - 1
    def drain():
        def wait_all(i):
            for t in range(S - 1):
                send(t, i).wait_send()
        loop(T, wait_all)

    if tuned:
        lax.fori_loop(lag, K + lag, gather_step, 0)
        near_local(0)
        lm_local(0)
        first_round(0)
        lax.fori_loop(K + lag, T - 1 + lag, gather_step, 0)
    else:
        lax.fori_loop(0, T - 1, gather_step, 0)
    last = H - 1
    if tuned:
        second_round(0)
    ready(T - 1)
    add_scores(T - 1)
    near_local(last, (lambda: near_first(last)) if tuned else lambda: None)
    add_logits(T - 1)
    if tuned:
        lm_local(last)
        one_round(last)
        near_second()
        two_rounds_end(0, share)
        early_mix()
        drain()
        one_round_end(last, share_out)
    else:
        lm_local(last)
        first_round(last)
        second_round(last)
        two_rounds_end(last, share_out)

    if not tuned:
        drain()
    for copy in token_sends + sends:
        copy.wait_send()


def mixture_kernel(logits, share, shift, out, last, early_sem, late_sem):
    H, S, RH = logits.shape[:3]
    G = max(1, 64 // RH)
    early = [
        pltpu.make_async_copy(logits.at[h, o], out.at[o, h], early_sem.at[h, o])
        for h in range(H - 1) for o in range(S)
    ]
    for copy in early:
        copy.start()

    def late_copy(n):
        span = pl.ds(n * G, G)
        return pltpu.make_async_copy(last.at[span], out.at[span, H - 1], late_sem.at[n])

    def tile(n, carry):
        span = pl.ds(n * G, G)
        last[span] = mix(logits[H - 1, span], share[span], shift[span, :, 0:1])
        late_copy(n).start()
        return carry

    def finish(n, carry):
        late_copy(n).wait()
        return carry

    lax.fori_loop(0, S // G, tile, 0)
    for copy in early:
        copy.wait()
    lax.fori_loop(0, S // G, finish, 0)


def body(S, V, hidden, lm_head, keys, values, licences, allowed):
    R, D = hidden.shape
    C = lm_head.shape[1]
    E = keys.shape[0]
    Q = allowed.shape[0]
    B = E // V
    H = 2 if S == 8 and V % 2 == 0 and R % 32 == 0 else 1
    RH = R // H
    QH = Q // H
    KC = math.gcd(D, DEPTH_CHUNK)
    K = D // KC
    T = H * K
    streams = S - 1
    hbm = pl.BlockSpec(memory_space=pltpu.HBM)
    vmem = pl.BlockSpec(memory_space=pltpu.VMEM)
    f32 = jnp.float32
    bf16 = jnp.bfloat16
    dma = pltpu.SemaphoreType.DMA
    logits, share, shift = pl.pallas_call(
        functools.partial(gather_kernel, S, V),
        out_shape=(
            pltpu.VMEM((H, S, RH, C), f32), pltpu.VMEM((S, RH, C), f32), pltpu.VMEM((S, RH, 128), f32)
        ),
        in_specs=[hbm] * 6,
        out_specs=(vmem, vmem, vmem),
        scratch_shapes=[
            pltpu.VMEM((H, S, K, RH, KC), hidden.dtype),
            pltpu.VMEM((K, KC, C), lm_head.dtype),
            pltpu.VMEM((K, E, KC), keys.dtype),
            pltpu.VMEM((1, E), jnp.int32),
            pltpu.VMEM((1, Q), jnp.int32),
            pltpu.VMEM((1, E), jnp.int32),
            pltpu.VMEM((H, E, QH), f32),
            pltpu.VMEM((E, 128), f32),
            pltpu.VMEM((H, E, QH), bf16),
            pltpu.VMEM((H, V, B, QH), bf16),
            pltpu.VMEM((E, QH), bf16),
            pltpu.VMEM((S, RH, C), f32),
            pltpu.VMEM((E, C), bf16),
            pltpu.VMEM((8, E), jnp.int32),
            pltpu.VMEM((V, 8, E), jnp.int32),
            pltpu.VMEM((E, 128), jnp.int32),
            pltpu.VMEM((Q, 128), jnp.int32),
            pltpu.VMEM((H, 2, QH), f32),
            pltpu.VMEM((S, 2, QH), f32),
            pltpu.VMEM((4, QH), f32),
            pltpu.VMEM((V, 4, QH), f32),
            pltpu.VMEM((S * V if H == 2 else 1, 1, QH), f32),
            pltpu.VMEM((1, QH), f32),
            pltpu.VMEM((1, QH), f32),
            pltpu.VMEM((S, 1, QH), f32),
            pltpu.VMEM((2, QH), f32),
            pltpu.VMEM((V, 2, QH), f32),
            dma((T,)), dma((K,)), dma((K,)), dma((3,)),
            dma((streams, T)), dma((streams, T)),
            dma((V - 1,)), dma((V - 1,)), dma((H, V - 1)), dma((H, V - 1)),
            dma((S - 1,)), dma((S - 1,)), dma((V - 1,)), dma((V - 1,)),
            dma((S * V - 1 if H == 2 else 1,)), dma((S * V - 1 if H == 2 else 1,)),
            dma((S - 1,)), dma((S - 1,)), dma((V - 1,)), dma((V - 1,)),
        ],
        compiler_params=pltpu.CompilerParams(
            collective_id=0, has_side_effects=True, vmem_limit_bytes=48 * 1024 * 1024
        ),
        name="gather_score",
    )(*[
        pltpu.with_memory_space_constraint(x, pltpu.HBM)
        for x in (hidden, lm_head, keys, values.reshape(1, E), licences.reshape(1, E), allowed.reshape(1, Q))
    ])

    return pl.pallas_call(
        mixture_kernel,
        out_shape=jax.ShapeDtypeStruct((S, H, RH, C), f32),
        in_specs=[vmem, vmem, vmem],
        out_specs=hbm,
        scratch_shapes=[pltpu.VMEM((S, RH, C), f32), dma((H, S)), dma((S,))],
        compiler_params=pltpu.CompilerParams(vmem_limit_bytes=8 * 1024 * 1024),
        name="mixture",
    )(logits, share, shift).reshape(Q, C)


def solution(mesh):
    return jax.shard_map(
        functools.partial(body, mesh.shape["store"], mesh.shape["vocab"]),
        mesh=mesh,
        in_specs=(
            P("store", None),
            P(None, ("store", "vocab")),
            P(("store", "vocab"), None),
            P(("store", "vocab")),
            P(("store", "vocab")),
            P(),
        ),
        out_specs=P(None, ("store", "vocab")),
        check_vma=False,
    )
```
